32 devices in a mesh: row: 16 (over z, x, core), col: 2 (over y).
Axes of the slice: x: 2, y: 2, z: 4, core: 2. Of those that a mesh axis runs over, the one named last changes fastest.
Arguments:
- amplitudes: float32 [16, 2, 1024, 1024], P('row', 'col'), may hold values from -6 to 6
- panels_left: bfloat16 [16, 2, 1024, 1024], P('row', None, 'col'), may hold values from -6 to 6
- panels_right: bfloat16 [2, 2, 1024, 1024], P('col', None, 'row'), may hold values from -6 to 6
- weights_right: bfloat16 [2, 2, 1024, 1024], P(None, 'col', 'row'), may hold values from -0.125 to 0.125
- weights_left: bfloat16 [2, 16, 1024, 1024], P(None, 'row', 'col'), may hold values from -0.125 to 0.125
- energy_left: float32 [16], P('row'), may hold values from -2 to -0.5
- energy_right: float32 [2], P('col'), may hold values from -2 to -0.5
- energy_virtual: float32 [1024], replicated, may hold values from 0.5 to 3
Outputs:
- updated: float32 [16, 2, 1024, 1024], P('row', 'col')
The draws below stay inside these ranges and needn't reach their ends.
All inputs are finite; a program needn't handle non-finite values.
Results may differ from the reference program's by a relative error of at most 0.0018.
Values may be sent and summed in bfloat16 or wider, within the bound.
No kernel may reach another device: no remote copies, remote signals or barrier semaphores. Data moves between devices by JAX's collectives and lax.ppermute only.
A program may use at most 128 MiB of HBM per device.

```python
import jax
import jax.numpy as jnp
from jax import lax

VIRT = 1024
PANELS = 2
LEFT = 16
RIGHT = 2


def steps_of(own_key, shape, split, least, high):
    def one(position, shards_of):
        draws = jax.random.uniform(jax.random.fold_in(jax.random.fold_in(own_key, 6), position), (shards_of,), jnp.float32, least / len(split), high / len(split))
        return jnp.repeat(jnp.exp(draws), shape[position] // shards_of).reshape((-1,) + (1,) * (len(shape) - position - 1))

    level = one(*split[0])
    for cut in split[1:]:
        level = level * one(*cut)
    return level


def gaussian(own_key, extent, scale, bound, shards=(), kind=jnp.bfloat16):
    loudness = steps_of(own_key, extent, shards, -0.22, 0.18) if shards else 1.0
    values = jax.random.normal(own_key, extent, jnp.float32) * scale * loudness
    return jnp.minimum(jnp.maximum(values, -bound), bound).astype(kind)


def setup_inputs(seed: int = 0) -> dict:
    key_of = jax.random.split(jax.random.key(seed), 9)
    return {
        "amplitudes": gaussian(key_of[0], (LEFT, RIGHT, VIRT, VIRT), 1.0, 6.0, ((0, 16), (1, 2)), jnp.float32),
        "panels_left": gaussian(key_of[1], (LEFT, PANELS, VIRT, VIRT), 1.0, 6.0, ((0, 16), (2, 2))),
        "panels_right": gaussian(key_of[2], (RIGHT, PANELS, VIRT, VIRT), 1.0, 6.0, ((0, 2), (2, 16))),
        "weights_right": gaussian(key_of[3], (PANELS, RIGHT, VIRT, VIRT), (PANELS * VIRT) ** -0.5, 0.125, ((1, 2), (2, 16))),
        "weights_left": gaussian(key_of[4], (PANELS, LEFT, VIRT, VIRT), (PANELS * VIRT) ** -0.5, 0.125, ((1, 16), (2, 2))),
        "energy_left": jnp.clip(-2.0 + 1.5 * jax.random.uniform(key_of[5], (LEFT,), jnp.float32) ** steps_of(key_of[5], (LEFT,), ((0, 16),), -0.2, 0.2), -2.0, -0.5),
        "energy_right": jnp.clip(-2.0 + 1.5 * jax.random.uniform(key_of[6], (RIGHT,), jnp.float32) ** steps_of(key_of[6], (RIGHT,), ((0, 2),), -0.2, 0.2), -2.0, -0.5),
        "energy_virtual": jnp.clip(jax.random.uniform(key_of[7], (VIRT,), jnp.float32, 0.5, 3.0), 0.5, 3.0),
    }


def combine_blocks(blocks):
    as_float = blocks.astype(jnp.float32)
    return (2.0 * as_float - jnp.swapaxes(as_float, -1, -2)).astype(jnp.bfloat16)


def reference(amplitudes, panels_left, panels_right, weights_right, weights_left, energy_left, energy_right, energy_virtual):
    left_mixed = combine_blocks(panels_left).astype(jnp.float32)
    right_mixed = combine_blocks(panels_right).astype(jnp.float32)
    right_float = weights_right.astype(jnp.float32)
    left_float = weights_left.astype(jnp.float32)
    virt_pair = energy_virtual[:, None] + energy_virtual[None, :]

    def one_left(index):
        direct = jnp.einsum("kac,kjcb->jab", left_mixed[index], right_float)
        weight_here = lax.dynamic_index_in_dim(left_float, index, 1, keepdims=False)
        mirror = jnp.einsum("jkac,kcb->jab", right_mixed, weight_here)
        residual = direct + jnp.swapaxes(mirror, 1, 2)
        denominator = energy_left[index] + energy_right[:, None, None] - virt_pair[None, :, :]
        return amplitudes[index] + residual / denominator

    return lax.map(one_left, jnp.arange(amplitudes.shape[0], dtype=jnp.int32))
```

```python
import functools

import jax
import jax.numpy as jnp
from jax import lax
from jax.experimental import pallas as pl
from jax.experimental.pallas import tpu as pltpu
from jax.sharding import PartitionSpec as P


F32 = jnp.float32
BF16 = jnp.bfloat16
TILE = 256


def any_specs(count):
    return [pl.BlockSpec(memory_space=pl.ANY)] * count


def vmem():
    return pl.BlockSpec(memory_space=pltpu.VMEM)


def cost(flops, moved):
    return pl.CostEstimate(flops=int(flops), bytes_accessed=int(moved), transcendentals=0)


def flipped(block):
    return jnp.transpose(block.astype(F32))


def turn_kernel(wl_ref, *out_refs):
    depth = wl_ref.shape[1]
    rows = out_refs[0].shape[0]
    for q, out_ref in enumerate(out_refs):
        for k in range(wl_ref.shape[0]):
            @pl.loop(0, rows // TILE)
            def _(s):
                at = pl.multiple_of(s * TILE, TILE)
                block = wl_ref[k, :, pl.ds(q * rows + at, TILE)]
                out_ref[pl.ds(at, TILE), pl.ds(k * depth, depth)] = flipped(block).astype(BF16)


def turn(wl, chunks):
    panels, depth, virt = wl.shape
    shape = jax.ShapeDtypeStruct((virt // chunks, panels * depth), BF16)
    return pl.pallas_call(
        turn_kernel,
        out_shape=[shape] * chunks,
        in_specs=[vmem()],
        out_specs=[vmem()] * chunks,
        cost_estimate=cost(0, 4 * wl.size),
        name="turn",
    )(wl)


def piece_rows(slot, outer, rows):
    steps, dx, dc = slot
    me = lax.axis_index("row")
    z, x, c = me // 4, (me // 2) % 2, me % 2
    z = lax.rem(z + outer - steps, outer)
    owner = z * 4 + (x ^ dx if not isinstance(dx, int) else (x if dx == 0 else 1 - x)) * 2 + (c if dc == 0 else 1 - c)
    return pl.multiple_of(owner * rows, rows)


def gather_copies(pieces, slots, outer, first, panels, dst, sem):
    out = []
    for n, (piece, slot) in enumerate(zip(pieces, slots)):
        rows = piece.shape[1]
        at = piece_rows(slot, outer, rows)
        out.append(
            pltpu.make_async_copy(piece.at[pl.ds(first, panels)], dst.at[:, pl.ds(at, rows), :], sem.at[n])
        )
    return out


def mirror_mix_kernel(slots, outer, panels, *refs):
    pieces = refs[: len(slots)]
    out_ref, right, sem = refs[len(slots):]
    copies = gather_copies(pieces, slots, outer, 0, panels, right, sem)
    for copy in copies:
        copy.start()
    for copy in copies:
        copy.wait()
    blocks = right.shape[1] // TILE
    for k in range(panels):
        @pl.loop(0, blocks * blocks)
        def _(s):
            up = pl.multiple_of((s // blocks) * TILE, TILE)
            along = pl.multiple_of((s % blocks) * TILE, TILE)
            across = flipped(right[k, pl.ds(along, TILE), pl.ds(up, TILE)])
            here = right[k, pl.ds(up, TILE), pl.ds(along, TILE)].astype(F32)
            out_ref[k, pl.ds(up, TILE), pl.ds(along, TILE)] = (2.0 * across - here).astype(BF16)


def mirror_mix(pieces, slots, outer, panels, virt):
    return pl.pallas_call(
        functools.partial(mirror_mix_kernel, slots, outer, panels),
        out_shape=jax.ShapeDtypeStruct((panels, virt, virt), BF16),
        in_specs=any_specs(len(slots)),
        out_specs=vmem(),
        scratch_shapes=[pltpu.VMEM((panels, virt, virt), BF16), pltpu.SemaphoreType.DMA((len(slots),))],
        cost_estimate=cost(0, 4 * panels * virt * virt),
        name="mirror_mix",
    )(*pieces)


def direct_kernel(slots, outer, panels, *refs):
    pieces = refs[: len(slots)]
    own_ref, other_ref, turned_ref, mixed_ref, out_ref, weight, left, sem, side = refs[len(slots):]
    virt = weight.shape[1]
    half = own_ref.shape[1]
    y = lax.axis_index("col")
    copies = gather_copies(pieces, slots, outer, panels, panels, weight, sem)
    mine = pl.multiple_of(y * half, half)
    theirs = pl.multiple_of((1 - y) * half, half)
    copies.append(pltpu.make_async_copy(own_ref, left.at[:, pl.ds(mine, half), :], side.at[0]))
    copies.append(pltpu.make_async_copy(other_ref, left.at[:, pl.ds(theirs, half), :], side.at[1]))
    for copy in copies:
        copy.start()
    for copy in copies:
        copy.wait()

    @pl.loop(0, virt // TILE)
    def _(s):
        at = pl.multiple_of(s * TILE, TILE)
        total = jnp.zeros((TILE, virt), F32)
        for k in range(panels):
            mixed = (
                2.0 * left[k, pl.ds(at, TILE), :].astype(F32) - flipped(left[k, :, pl.ds(at, TILE)])
            ).astype(BF16)
            total += jnp.dot(mixed, weight[k], preferred_element_type=F32)
            total += jnp.dot(
                turned_ref[pl.ds(at, TILE), pl.ds(k * half, half)],
                mixed_ref[k, pl.ds(mine, half), :],
                preferred_element_type=F32,
            )
        out_ref[pl.ds(at, TILE), :] = total


def direct_part(pieces, slots, outer, own, other, turned, mixed):
    panels, half, virt = own.shape
    return pl.pallas_call(
        functools.partial(direct_kernel, slots, outer, panels),
        out_shape=jax.ShapeDtypeStruct((virt, virt), F32),
        in_specs=any_specs(len(slots) + 2) + [vmem(), vmem()],
        out_specs=vmem(),
        scratch_shapes=[
            pltpu.VMEM((panels, virt, virt), BF16),
            pltpu.VMEM((panels, virt, virt), BF16),
            pltpu.SemaphoreType.DMA((len(slots),)),
            pltpu.SemaphoreType.DMA((2,)),
        ],
        cost_estimate=cost(3 * panels * virt**3, 14 * virt * virt),
        name="direct_part",
    )(*pieces, own, other, turned, mixed)


def finish_kernel(half, el_ref, er_ref, evr_ref, evc_ref, base_ref, amp_ref, came_ref, mixed_ref, *rest):
    out_ref = rest[-1]
    total = base_ref[...]
    for k in range(mixed_ref.shape[0]):
        total += jnp.dot(came_ref[:, pl.ds(k * half, half)], mixed_ref[k], preferred_element_type=F32)
    pair = evc_ref[...] + evr_ref[...]
    out_ref[...] = amp_ref[...] + total / (el_ref[0] + er_ref[0] - pair)


def finish(q, chunks, el, er, evr, evc, base, amp, came, mixed, held):
    virt = base.shape[0]
    panels = mixed.shape[0]
    half = virt // 2
    rows = virt // chunks
    smem = pl.BlockSpec(memory_space=pltpu.SMEM)
    stripe = pl.BlockSpec((rows, virt), lambda s: (q, 0))
    in_specs = [
        smem,
        smem,
        pl.BlockSpec((1, virt), lambda s: (0, 0)),
        pl.BlockSpec((rows, 1), lambda s: (q, 0)),
        stripe,
        stripe,
        pl.BlockSpec((rows, panels * half), lambda s: (0, 0)),
        pl.BlockSpec((panels, half, virt), lambda s: (0, 1 - lax.axis_index("col"), 0)),
    ]
    args = [el, er, evr, evc, base, amp, came, mixed]
    aliases = {}
    if held is not None:
        in_specs.append(pl.BlockSpec(memory_space=pl.ANY))
        args.append(held)
        aliases = {len(args) - 1: 0}
    return pl.pallas_call(
        functools.partial(finish_kernel, half),
        grid=(1,),
        out_shape=jax.ShapeDtypeStruct((virt, virt), F32),
        in_specs=in_specs,
        out_specs=stripe,
        input_output_aliases=aliases,
        cost_estimate=cost(panels * rows * virt * virt, 12 * rows * virt + 4 * half * virt),
        name="finish",
    )(*args)


def exchange_body(
    sizes,
    amplitudes,
    panels_left,
    panels_right,
    weights_right,
    weights_left,
    energy_left,
    energy_right,
    energy_virtual,
):
    n, chunks = sizes
    outer = n // 4
    own = panels_left[0]
    panels, _, virt = own.shape

    def over_col(block):
        return lax.ppermute(block, "col", [(0, 1), (1, 0)])

    def over_row(block, where):
        return lax.ppermute(block, "row", [(r, where(r)) for r in range(n)])

    shard = jnp.concatenate([panels_right[0], weights_right[:, 0]], axis=0)
    other = over_col(own)
    turned = turn(weights_left[:, 0], chunks)
    came = [over_col(block) for block in turned]
    pieces, slots = [], []
    for steps in range(outer):
        piece = shard if steps == 0 else over_row(shard, lambda r: (r + 4 * steps) % n)
        across = over_row(piece, lambda r: r ^ 2)
        for dx, block in enumerate((piece, across)):
            pieces += [block, over_row(block, lambda r: r ^ 1)]
            slots += [(steps, dx, 0), (steps, dx, 1)]
    mixed = mirror_mix(pieces, slots, outer, panels, virt)
    base = direct_part(pieces, slots, outer, own, other, jnp.concatenate(turned, axis=0), mixed)
    out = None
    for q in range(chunks):
        out = finish(
            q,
            chunks,
            energy_left,
            energy_right,
            energy_virtual[None, :],
            energy_virtual[:, None],
            base,
            amplitudes[0, 0],
            came[q],
            mixed,
            out,
        )
    return out[None, None]


def combine_blocks(blocks):
    as_float = blocks.astype(F32)
    return (2.0 * as_float - jnp.swapaxes(as_float, -1, -2)).astype(BF16)


def gather_body(
    amplitudes,
    panels_left,
    panels_right,
    weights_right,
    weights_left,
    energy_left,
    energy_right,
    energy_virtual,
):
    left_mixed = combine_blocks(lax.all_gather(panels_left[0], "col", axis=1, tiled=True))
    right_mixed = combine_blocks(lax.all_gather(panels_right[0], "row", axis=1, tiled=True))
    weight_right = lax.all_gather(weights_right[:, 0], "row", axis=1, tiled=True)
    weight_left = lax.all_gather(weights_left[:, 0], "col", axis=1, tiled=True)
    direct = jnp.einsum("kac,kcb->ab", left_mixed, weight_right, preferred_element_type=F32)
    mirror = jnp.einsum("kac,kcb->ab", right_mixed, weight_left, preferred_element_type=F32)
    residual = direct + jnp.transpose(mirror)
    virt_pair = energy_virtual[:, None] + energy_virtual[None, :]
    denominator = energy_left[0] + energy_right[0] - virt_pair
    return (amplitudes[0, 0] + residual / denominator)[None, None]


def solution(mesh):
    n, m = mesh.shape["row"], mesh.shape["col"]
    placed = (
        P("row", "col", None, None),
        P("row", None, "col", None),
        P("col", None, "row", None),
        P(None, "col", "row", None),
        P(None, "row", "col", None),
        P("row"),
        P("col"),
        P(),
    )
    body = functools.partial(exchange_body, (n, 4)) if m == 2 and n % 4 == 0 else gather_body
    return jax.shard_map(
        body, mesh=mesh, in_specs=placed, out_specs=P("row", "col", None, None), check_vma=False
    )
```

```python
import functools

import jax
import jax.numpy as jnp
from jax import lax
from jax.experimental import pallas as pl
from jax.experimental.pallas import tpu as pltpu
from jax.sharding import PartitionSpec as P


F32 = jnp.float32
BF16 = jnp.bfloat16
TILE = 256
WIDE = 60


def tile_of(rows):
    return TILE if rows % TILE == 0 else TILE // 2


def any_specs(count):
    return [pl.BlockSpec(memory_space=pl.ANY)] * count


def vmem():
    return pl.BlockSpec(memory_space=pltpu.VMEM)


def cost(flops, moved):
    return pl.CostEstimate(flops=int(flops), bytes_accessed=int(moved), transcendentals=0)


def limit(mib):
    return pltpu.CompilerParams(vmem_limit_bytes=mib << 20)


def flipped(block):
    return jnp.transpose(block)


def turn_kernel(wl_ref, *out_refs):
    depth = wl_ref.shape[1]
    first = 0
    for out_ref in out_refs:
        rows = out_ref.shape[0]
        tile = tile_of(rows)
        for k in range(wl_ref.shape[0]):
            @pl.loop(0, rows // tile)
            def _(s):
                at = pl.multiple_of(s * tile, tile)
                block = wl_ref[k, :, pl.ds(first + at, tile)]
                out_ref[pl.ds(at, tile), pl.ds(k * depth, depth)] = flipped(block)
        first += rows


def turn(wl, heights):
    panels, depth, _ = wl.shape
    return pl.pallas_call(
        turn_kernel,
        out_shape=[jax.ShapeDtypeStruct((rows, panels * depth), BF16) for rows in heights],
        in_specs=[vmem()],
        out_specs=[vmem()] * len(heights),
        compiler_params=limit(8),
        cost_estimate=cost(0, 4 * wl.size),
        name="turn",
    )(wl)


def gather_copies(pieces, dst, sem):
    me = lax.axis_index("row")
    out = []
    for n, piece in enumerate(pieces):
        rows = piece.shape[1]
        at = pl.multiple_of((me ^ n) * rows, rows)
        out.append(pltpu.make_async_copy(piece, dst.at[:, pl.ds(at, rows), :], sem.at[n]))
    return out


def hbm():
    return pl.BlockSpec(memory_space=pltpu.HBM)


def mirror_mix_kernel(*refs):
    *pieces, mine_ref, theirs_ref, right, mixed, sem, side = refs
    panels, virt, _ = right.shape
    half = virt // 2
    y = lax.axis_index("col")
    mine = pl.multiple_of(y * half, half)
    theirs = pl.multiple_of((1 - y) * half, half)
    copies = gather_copies(pieces, right, sem)
    for copy in copies:
        copy.start()
    for copy in copies:
        copy.wait()
    blocks = virt // TILE
    out = []
    for k in range(panels):
        @pl.loop(0, blocks * blocks)
        def _(s):
            up = pl.multiple_of((s // blocks) * TILE, TILE)
            along = pl.multiple_of((s % blocks) * TILE, TILE)
            across = flipped(right[k, pl.ds(along, TILE), pl.ds(up, TILE)]).astype(F32)
            here = right[k, pl.ds(up, TILE), pl.ds(along, TILE)].astype(F32)
            mixed[k, pl.ds(up, TILE), pl.ds(along, TILE)] = (2.0 * across - here).astype(BF16)

        for n, (at, dst) in enumerate(((mine, mine_ref), (theirs, theirs_ref))):
            out.append(
                pltpu.make_async_copy(mixed.at[k, pl.ds(at, half), :], dst.at[k], side.at[2 * k + n])
            )
            out[-1].start()
    for copy in out:
        copy.wait()


def mirror_mix(pieces, panels, virt):
    return pl.pallas_call(
        mirror_mix_kernel,
        out_shape=[jax.ShapeDtypeStruct((panels, virt // 2, virt), BF16)] * 2,
        in_specs=any_specs(len(pieces)),
        out_specs=[hbm(), hbm()],
        scratch_shapes=[
            pltpu.VMEM((panels, virt, virt), BF16),
            pltpu.VMEM((panels, virt, virt), BF16),
            pltpu.SemaphoreType.DMA((len(pieces),)),
            pltpu.SemaphoreType.DMA((2 * panels,)),
        ],
        compiler_params=limit(WIDE),
        cost_estimate=cost(0, 8 * virt * virt),
        name="mirror_mix",
    )(*pieces)


def direct_kernel(heights, *refs):
    *refs, own_ref, other_ref, mine_ref, out_ref, weight, own, other, mixed, turned, sem, came, side = refs
    pieces, blocks = refs[: -len(heights)], refs[-len(heights):]
    panels, virt, _ = weight.shape
    half = virt // 2
    first = [pltpu.make_async_copy(mine_ref, mixed, side.at[0])]
    at = 0
    for n, (rows, block) in enumerate(zip(heights, blocks)):
        first.append(pltpu.make_async_copy(block, turned.at[pl.ds(at, rows)], came.at[n]))
        at += rows
    then = gather_copies(pieces, weight, sem)
    then.append(pltpu.make_async_copy(own_ref, own, side.at[1]))
    then.append(pltpu.make_async_copy(other_ref, other, side.at[2]))
    for copy in first + then:
        copy.start()
    for copy in first:
        copy.wait()

    @pl.loop(0, virt // TILE)
    def _(s):
        span = pl.ds(pl.multiple_of(s * TILE, TILE), TILE)
        part = jnp.zeros((TILE, virt), F32)
        for k in range(panels):
            part += jnp.dot(turned[span, pl.ds(k * half, half)], mixed[k], preferred_element_type=F32)
        out_ref[span, :] = part

    for copy in then:
        copy.wait()
    y = lax.axis_index("col")
    mine = pl.multiple_of(y * half, half)
    theirs = pl.multiple_of((1 - y) * half, half)
    for rows_ref, start in ((own, mine), (other, theirs)):
        @pl.loop(0, half // TILE)
        def _(s):
            at = pl.multiple_of(s * TILE, TILE)
            span = pl.ds(pl.multiple_of(start + at, TILE), TILE)
            part = out_ref[span, :]
            for k in range(panels):
                for columns_ref, inner in ((own, mine), (other, theirs)):
                    here = rows_ref[k, pl.ds(at, TILE), pl.ds(inner, half)].astype(F32)
                    across = flipped(columns_ref[k, :, span]).astype(F32)
                    left = (2.0 * here - across).astype(BF16)
                    part += jnp.dot(left, weight[k, pl.ds(inner, half), :], preferred_element_type=F32)
            out_ref[span, :] = part


def direct_part(pieces, heights, turned, own, other, mine):
    panels, half, virt = own.shape
    side = pltpu.VMEM((panels, half, virt), BF16)
    return pl.pallas_call(
        functools.partial(direct_kernel, heights),
        out_shape=jax.ShapeDtypeStruct((virt, virt), F32),
        in_specs=any_specs(len(pieces) + len(heights) + 3),
        out_specs=vmem(),
        scratch_shapes=[
            pltpu.VMEM((panels, virt, virt), BF16),
            side,
            side,
            side,
            pltpu.VMEM((virt, panels * half), BF16),
            pltpu.SemaphoreType.DMA((len(pieces),)),
            pltpu.SemaphoreType.DMA((len(heights),)),
            pltpu.SemaphoreType.DMA((3,)),
        ],
        compiler_params=limit(24),
        cost_estimate=cost(3 * panels * virt**3, 14 * virt * virt),
        name="direct_part",
    )(*pieces, *turned, own, other, mine)


def finish_kernel(first, el_ref, er_ref, evr_ref, evc_ref, base_ref, amp_ref, came_ref, mixed_ref, *rest):
    out_ref, done, sem = rest[-3:]
    panels, half, _ = mixed_ref.shape
    rows = came_ref.shape[0]
    level = el_ref[0] + er_ref[0]
    tile = tile_of(rows)
    copies = []
    for at in range(0, rows, tile):
        total = base_ref[pl.ds(first + at, tile), :]
        for k in range(panels):
            total += jnp.dot(
                came_ref[pl.ds(at, tile), pl.ds(k * half, half)],
                mixed_ref[k],
                preferred_element_type=F32,
            )
        pair = evc_ref[pl.ds(first + at, tile), :] + evr_ref[...]
        done[pl.ds(at, tile), :] = amp_ref[pl.ds(first + at, tile), :] + total / (level - pair)
        copies.append(
            pltpu.make_async_copy(
                done.at[pl.ds(at, tile)], out_ref.at[pl.ds(first + at, tile)], sem.at[at // tile]
            )
        )
        copies[-1].start()
    for copy in copies:
        copy.wait()


def finish(first, el, er, evr, evc, base, amp, came, mixed, held):
    virt = base.shape[0]
    panels = mixed.shape[0]
    rows = came.shape[0]
    smem = pl.BlockSpec(memory_space=pltpu.SMEM)
    in_specs = [smem] * 2 + [vmem()] * 6
    args = [el, er, evr, evc, base, amp, came, mixed]
    aliases = {}
    if held is not None:
        in_specs.append(pl.BlockSpec(memory_space=pl.ANY))
        args.append(held)
        aliases = {len(args) - 1: 0}
    return pl.pallas_call(
        functools.partial(finish_kernel, first),
        out_shape=jax.ShapeDtypeStruct((virt, virt), F32),
        in_specs=in_specs,
        out_specs=pl.BlockSpec(memory_space=pl.ANY),
        input_output_aliases=aliases,
        scratch_shapes=[pltpu.VMEM((rows, virt), F32), pltpu.SemaphoreType.DMA((rows // tile_of(rows),))],
        compiler_params=limit(8),
        cost_estimate=cost(panels * rows * virt * virt, 12 * rows * virt + 4 * virt * virt),
        name="finish",
    )(*args)


def exchange_body(
    amplitudes,
    panels_left,
    panels_right,
    weights_right,
    weights_left,
    energy_left,
    energy_right,
    energy_virtual,
):
    n = lax.axis_size("row")
    own = panels_left[0]
    panels, _, virt = own.shape
    heights = (virt // 2, 3 * virt // 8, virt // 8)

    def over_col(block):
        return lax.ppermute(block, "col", [(0, 1), (1, 0)])

    def over_row(block, across, steps=range(4)):
        return lax.ppermute(block, "row", [(r, r ^ across) for r in range(n) if r // 4 in steps])

    other = over_col(own)
    turned = turn(weights_left[:, 0], heights)
    came = [over_col(block) for block in turned]
    inner = (lax.axis_index("row") // 4) % 3 > 0
    gathered = []
    for shard in (panels_right[0], weights_right[:, 0]):
        by_step = [shard, over_row(shard, 4), over_row(shard, 8)]
        middle = over_row(shard, 12, (1, 2))
        ends = over_row(by_step[2], 4, (1, 2))
        by_step.append(jnp.where(inner, middle, ends))
        pieces = []
        for piece in by_step:
            across = over_row(piece, 2)
            for block in (piece, across):
                pieces += [block, over_row(block, 1)]
        gathered.append(pieces)
    mine, mixed = mirror_mix(gathered[0], panels, virt)
    base = direct_part(gathered[1], heights, turned, own, other, mine)
    out = None
    first = 0
    for rows, block in zip(heights, came):
        out = finish(
            first,
            energy_left,
            energy_right,
            energy_virtual[None, :],
            energy_virtual[:, None],
            base,
            amplitudes[0, 0],
            block,
            mixed,
            out,
        )
        first += rows
    return out[None, None]


def combine_blocks(blocks):
    as_float = blocks.astype(F32)
    return (2.0 * as_float - jnp.swapaxes(as_float, -1, -2)).astype(BF16)


def gather_body(
    amplitudes,
    panels_left,
    panels_right,
    weights_right,
    weights_left,
    energy_left,
    energy_right,
    energy_virtual,
):
    left_mixed = combine_blocks(lax.all_gather(panels_left[0], "col", axis=1, tiled=True))
    right_mixed = combine_blocks(lax.all_gather(panels_right[0], "row", axis=1, tiled=True))
    weight_right = lax.all_gather(weights_right[:, 0], "row", axis=1, tiled=True)
    weight_left = lax.all_gather(weights_left[:, 0], "col", axis=1, tiled=True)
    direct = jnp.einsum("kac,kcb->ab", left_mixed, weight_right, preferred_element_type=F32)
    mirror = jnp.einsum("kac,kcb->ab", right_mixed, weight_left, preferred_element_type=F32)
    residual = direct + jnp.transpose(mirror)
    virt_pair = energy_virtual[:, None] + energy_virtual[None, :]
    denominator = energy_left[0] + energy_right[0] - virt_pair
    return (amplitudes[0, 0] + residual / denominator)[None, None]


def solution(mesh):
    n, m = mesh.shape["row"], mesh.shape["col"]
    placed = (
        P("row", "col", None, None),
        P("row", None, "col", None),
        P("col", None, "row", None),
        P(None, "col", "row", None),
        P(None, "row", "col", None),
        P("row"),
        P("col"),
        P(),
    )
    exchanged = m == 2 and n == 16
    return jax.shard_map(
        exchange_body if exchanged else gather_body,
        mesh=mesh,
        in_specs=placed,
        out_specs=P("row", "col", None, None),
        check_vma=False,
    )
```

```python
import functools

import jax
import jax.numpy as jnp
from jax import lax
from jax.experimental import pallas as pl
from jax.experimental.pallas import tpu as pltpu
from jax.sharding import PartitionSpec as P


F32 = jnp.float32
BF16 = jnp.bfloat16
TILE = 256
WIDE = 60
STRIP = 256


def tile_of(rows):
    return TILE if rows % TILE == 0 else TILE // 2


def any_specs(count):
    return [pl.BlockSpec(memory_space=pl.ANY)] * count


def vmem():
    return pl.BlockSpec(memory_space=pltpu.VMEM)


def cost(flops, moved):
    return pl.CostEstimate(flops=int(flops), bytes_accessed=int(moved), transcendentals=0)


def limit(mib):
    return pltpu.CompilerParams(vmem_limit_bytes=mib << 20)


def flipped(block):
    return jnp.transpose(block)


def turn_kernel(early, tail, wl_ref, early_ref, most_ref, last_ref):
    panels, depth, virt = wl_ref.shape
    main, part = virt - tail, tail // panels
    for k in range(panels):
        for out_ref, first, rows in ((early_ref, 0, early), (most_ref, early, main - early)):
            tile = tile_of(rows)

            @pl.loop(0, rows // tile)
            def _(s):
                at = pl.multiple_of(s * tile, tile)
                block = wl_ref[k, :, pl.ds(first + at, tile)]
                out_ref[pl.ds(at, tile), pl.ds(k * depth, depth)] = flipped(block)

        block = flipped(wl_ref[k, :, pl.ds(main, tail)])
        dst, at = (last_ref, 0) if k == panels - 1 else (most_ref, main - early + k * part)
        for g in range(panels):
            dst[pl.ds(at, part), pl.ds(g * depth, depth)] = block[g * part:(g + 1) * part]


def turn(wl, early, tail):
    panels, depth, virt = wl.shape
    part = tail // panels
    return pl.pallas_call(
        functools.partial(turn_kernel, early, tail),
        out_shape=[jax.ShapeDtypeStruct((rows, panels * depth), BF16) for rows in (early, virt - early - part, part)],
        in_specs=[vmem()],
        out_specs=[vmem()] * 3,
        compiler_params=limit(8),
        cost_estimate=cost(0, 4 * wl.size),
        name="turn",
    )(wl)


def packed(ref, at, part, panels, depth):
    rows = [ref[pl.ds(at, part), pl.ds(g * depth, depth)] for g in range(panels)]
    return jnp.concatenate(rows, axis=0)


def gather_copies(pieces, dst, sem):
    me = lax.axis_index("row")
    out = []
    for n, piece in enumerate(pieces):
        rows = piece.shape[1]
        at = pl.multiple_of((me ^ n) * rows, rows)
        out.append(pltpu.make_async_copy(piece, dst.at[:, pl.ds(at, rows), :], sem.at[n]))
    return out


def hbm():
    return pl.BlockSpec(memory_space=pltpu.HBM)


def mirror_mix_kernel(*refs):
    *pieces, mine_ref, theirs_ref, right, mixed, sem, side = refs
    panels, virt, _ = right.shape
    half = virt // 2
    y = lax.axis_index("col")
    mine = pl.multiple_of(y * half, half)
    theirs = pl.multiple_of((1 - y) * half, half)
    copies = gather_copies(pieces, right, sem)
    for copy in copies:
        copy.start()
    for copy in copies:
        copy.wait()
    blocks = virt // TILE
    out = []
    for k in range(panels):
        @pl.loop(0, blocks * blocks)
        def _(s):
            up = pl.multiple_of((s // blocks) * TILE, TILE)
            along = pl.multiple_of((s % blocks) * TILE, TILE)
            across = flipped(right[k, pl.ds(along, TILE), pl.ds(up, TILE)]).astype(F32)
            here = right[k, pl.ds(up, TILE), pl.ds(along, TILE)].astype(F32)
            mixed[k, pl.ds(up, TILE), pl.ds(along, TILE)] = (2.0 * across - here).astype(BF16)

        for n, (at, dst) in enumerate(((mine, mine_ref), (theirs, theirs_ref))):
            out.append(
                pltpu.make_async_copy(mixed.at[k, pl.ds(at, half), :], dst.at[k], side.at[2 * k + n])
            )
            out[-1].start()
    for copy in out:
        copy.wait()


def mirror_mix(pieces, panels, virt):
    return pl.pallas_call(
        mirror_mix_kernel,
        out_shape=[jax.ShapeDtypeStruct((panels, virt // 2, virt), BF16)] * 2,
        in_specs=any_specs(len(pieces)),
        out_specs=[hbm(), hbm()],
        scratch_shapes=[
            pltpu.VMEM((panels, virt, virt), BF16),
            pltpu.VMEM((panels, virt, virt), BF16),
            pltpu.SemaphoreType.DMA((len(pieces),)),
            pltpu.SemaphoreType.DMA((2 * panels,)),
        ],
        compiler_params=limit(WIDE),
        cost_estimate=cost(0, 8 * virt * virt),
        name="mirror_mix",
    )(*pieces)


def direct_kernel(early, tail, *refs):
    *refs, own_ref, other_ref, mine_ref, out_ref, weight, own, other, mixed, turned, sem, came, side = refs
    *pieces, early_ref, most_ref, last_ref = refs
    panels, virt, _ = weight.shape
    half = virt // 2
    main, part = virt - tail, tail // panels
    first = [
        pltpu.make_async_copy(mine_ref, mixed, side.at[0]),
        pltpu.make_async_copy(early_ref, turned.at[pl.ds(0, early)], side.at[3]),
        pltpu.make_async_copy(
            most_ref.at[pl.ds(0, main - early)], turned.at[pl.ds(early, main - early)], side.at[4]
        ),
    ]
    for k in range(panels):
        src, at = (last_ref, 0) if k == panels - 1 else (most_ref, main - early + k * part)
        for g in range(panels):
            first.append(
                pltpu.make_async_copy(
                    src.at[pl.ds(at, part), pl.ds(g * half, half)],
                    turned.at[pl.ds(main + g * part, part), pl.ds(k * half, half)],
                    came.at[k * panels + g],
                )
            )
    then = gather_copies(pieces, weight, sem)
    then.append(pltpu.make_async_copy(own_ref, own, side.at[1]))
    then.append(pltpu.make_async_copy(other_ref, other, side.at[2]))
    for copy in first + then:
        copy.start()
    for copy in first:
        copy.wait()

    @pl.loop(0, virt // TILE)
    def _(s):
        span = pl.ds(pl.multiple_of(s * TILE, TILE), TILE)
        part = jnp.zeros((TILE, virt), F32)
        for k in range(panels):
            part += jnp.dot(turned[span, pl.ds(k * half, half)], mixed[k], preferred_element_type=F32)
        out_ref[span, :] = part

    for copy in then:
        copy.wait()
    y = lax.axis_index("col")
    mine = pl.multiple_of(y * half, half)
    theirs = pl.multiple_of((1 - y) * half, half)
    for rows_ref, start in ((own, mine), (other, theirs)):
        @pl.loop(0, half // TILE)
        def _(s):
            at = pl.multiple_of(s * TILE, TILE)
            span = pl.ds(pl.multiple_of(start + at, TILE), TILE)
            part = out_ref[span, :]
            for k in range(panels):
                for columns_ref, inner in ((own, mine), (other, theirs)):
                    here = rows_ref[k, pl.ds(at, TILE), pl.ds(inner, half)].astype(F32)
                    across = flipped(columns_ref[k, :, span]).astype(F32)
                    left = (2.0 * here - across).astype(BF16)
                    part += jnp.dot(left, weight[k, pl.ds(inner, half), :], preferred_element_type=F32)
            out_ref[span, :] = part


def direct_part(pieces, early, tail, turned, own, other, mine):
    panels, half, virt = own.shape
    side = pltpu.VMEM((panels, half, virt), BF16)
    return pl.pallas_call(
        functools.partial(direct_kernel, early, tail),
        out_shape=jax.ShapeDtypeStruct((virt, virt), F32),
        in_specs=any_specs(len(pieces) + 6),
        out_specs=vmem(),
        scratch_shapes=[
            pltpu.VMEM((panels, virt, virt), BF16),
            side,
            side,
            side,
            pltpu.VMEM((virt, panels * half), BF16),
            pltpu.SemaphoreType.DMA((len(pieces),)),
            pltpu.SemaphoreType.DMA((panels * panels,)),
            pltpu.SemaphoreType.DMA((5,)),
        ],
        compiler_params=limit(24),
        cost_estimate=cost(3 * panels * virt**3, 14 * virt * virt),
        name="direct_part",
    )(*pieces, *turned, own, other, mine)


def update_rows(level, evr_ref, evc_ref, amp_ref, out_ref, done, sem, first, spans, product):
    virt = out_ref.shape[1]
    copies = []
    for n, (at, rows) in enumerate(spans):
        here, whole = pl.ds(at, rows), pl.ds(first + at, rows)
        down = evc_ref[whole, :]
        for along in range(0, virt, STRIP):
            strip = pl.ds(along, STRIP)
            pair = down + evr_ref[:, strip]
            done[here, strip] = amp_ref[whole, strip] + product(at, rows, strip) / (level - pair)
            copies.append(
                pltpu.make_async_copy(
                    done.at[here, strip], out_ref.at[whole, strip], sem.at[n, along // STRIP]
                )
            )
            copies[-1].start()
    return copies


def some_kernel(first, tail, el_ref, er_ref, evr_ref, evc_ref, base_ref, amp_ref, came_ref, mixed_ref, *rest):
    rest = rest[1:] if first else rest
    out_ref, *more, done, sem = rest
    panels, half, virt = mixed_ref.shape
    rows = done.shape[0]
    tile = tile_of(rows)

    def product(at, count, strip):
        total = base_ref[pl.ds(first + at, count), strip]
        for k in range(panels):
            total += jnp.dot(
                came_ref[pl.ds(at, count), pl.ds(k * half, half)],
                mixed_ref[k, :, strip],
                preferred_element_type=F32,
            )
        return total

    spans = [(at, tile) for at in range(0, rows, tile)]
    level = el_ref[0] + er_ref[0]
    copies = update_rows(level, evr_ref, evc_ref, amp_ref, out_ref, done, sem, first, spans, product)
    if more:
        part = tail // panels
        left = base_ref[pl.ds(virt - tail, tail), :]
        for k in range(panels - 1):
            block = packed(came_ref, rows + k * part, part, panels, half)
            left += jnp.dot(block, mixed_ref[k], preferred_element_type=F32)
        more[0][...] = left
    for copy in copies:
        copy.wait()


def last_kernel(
    tail, el_ref, er_ref, evr_ref, evc_ref, rest_ref, amp_ref, came_ref, mixed_ref, held_ref, out_ref, done, sem
):
    panels, half, virt = mixed_ref.shape
    came = packed(came_ref, 0, tail // panels, panels, half)

    def product(at, rows, strip):
        here = mixed_ref[panels - 1, :, strip]
        return rest_ref[:, strip] + jnp.dot(came, here, preferred_element_type=F32)

    level = el_ref[0] + er_ref[0]
    copies = update_rows(
        level, evr_ref, evc_ref, amp_ref, out_ref, done, sem, virt - tail, [(0, tail)], product
    )
    for copy in copies:
        copy.wait()


def finish(early, tail, energies, base, amp, came, mixed):
    panels, _, virt = mixed.shape
    smem = pl.BlockSpec(memory_space=pltpu.SMEM)
    in_specs = [smem] * 2 + [vmem()] * 6
    main = virt - tail
    whole = jax.ShapeDtypeStruct((virt, virt), F32)
    strips = virt // STRIP
    rest = jax.ShapeDtypeStruct((tail, virt), F32)
    out = None
    for n, (first, rows) in enumerate(((0, early), (early, main - early))):
        out = pl.pallas_call(
            functools.partial(some_kernel, first, tail),
            out_shape=[whole, rest] if n else whole,
            in_specs=in_specs + any_specs(n),
            out_specs=[pl.BlockSpec(memory_space=pl.ANY), vmem()] if n else pl.BlockSpec(memory_space=pl.ANY),
            input_output_aliases={8: 0} if n else {},
            scratch_shapes=[
                pltpu.VMEM((rows, virt), F32),
                pltpu.SemaphoreType.DMA((rows // tile_of(rows), strips)),
            ],
            compiler_params=limit(8),
            cost_estimate=cost(panels * rows * virt * virt, 12 * rows * virt + 4 * virt * virt),
            name="finish_some",
        )(*energies, base, amp, came[n], mixed, *([out] if n else []))
    out, rest = out
    return pl.pallas_call(
        functools.partial(last_kernel, tail),
        out_shape=whole,
        in_specs=in_specs + [pl.BlockSpec(memory_space=pl.ANY)],
        out_specs=pl.BlockSpec(memory_space=pl.ANY),
        input_output_aliases={8: 0},
        scratch_shapes=[pltpu.VMEM((tail, virt), F32), pltpu.SemaphoreType.DMA((1, strips))],
        compiler_params=limit(8),
        cost_estimate=cost(tail * virt * virt, 12 * tail * virt + 2 * virt * virt),
        name="finish_last",
    )(*energies, rest, amp, came[2], mixed, out)


def exchange_body(
    amplitudes,
    panels_left,
    panels_right,
    weights_right,
    weights_left,
    energy_left,
    energy_right,
    energy_virtual,
):
    n = lax.axis_size("row")
    own = panels_left[0]
    panels, _, virt = own.shape
    tail = virt // 8
    early = 3 * virt // 4

    def over_col(block):
        return lax.ppermute(block, "col", [(0, 1), (1, 0)])

    def over_row(block, across, steps=range(4)):
        return lax.ppermute(block, "row", [(r, r ^ across) for r in range(n) if r // 4 in steps])

    other = over_col(own)
    turned = turn(weights_left[:, 0], early, tail)
    came = [over_col(block) for block in turned]
    inner = (lax.axis_index("row") // 4) % 3 > 0
    gathered = []
    for shard in (panels_right[0], weights_right[:, 0]):
        by_step = [shard, over_row(shard, 4), over_row(shard, 8)]
        middle = over_row(shard, 12, (1, 2))
        ends = over_row(by_step[2], 4, (1, 2))
        by_step.append(jnp.where(inner, middle, ends))
        pieces = []
        for piece in by_step:
            across = over_row(piece, 2)
            for block in (piece, across):
                pieces += [block, over_row(block, 1)]
        gathered.append(pieces)
    mine, mixed = mirror_mix(gathered[0], panels, virt)
    base = direct_part(gathered[1], early, tail, turned, own, other, mine)
    energies = (energy_left, energy_right, energy_virtual[None, :], energy_virtual[:, None])
    out = finish(early, tail, energies, base, amplitudes[0, 0], came, mixed)
    return out[None, None]


def combine_blocks(blocks):
    as_float = blocks.astype(F32)
    return (2.0 * as_float - jnp.swapaxes(as_float, -1, -2)).astype(BF16)


def gather_body(
    amplitudes,
    panels_left,
    panels_right,
    weights_right,
    weights_left,
    energy_left,
    energy_right,
    energy_virtual,
):
    left_mixed = combine_blocks(lax.all_gather(panels_left[0], "col", axis=1, tiled=True))
    right_mixed = combine_blocks(lax.all_gather(panels_right[0], "row", axis=1, tiled=True))
    weight_right = lax.all_gather(weights_right[:, 0], "row", axis=1, tiled=True)
    weight_left = lax.all_gather(weights_left[:, 0], "col", axis=1, tiled=True)
    direct = jnp.einsum("kac,kcb->ab", left_mixed, weight_right, preferred_element_type=F32)
    mirror = jnp.einsum("kac,kcb->ab", right_mixed, weight_left, preferred_element_type=F32)
    residual = direct + jnp.transpose(mirror)
    virt_pair = energy_virtual[:, None] + energy_virtual[None, :]
    denominator = energy_left[0] + energy_right[0] - virt_pair
    return (amplitudes[0, 0] + residual / denominator)[None, None]


def solution(mesh):
    n, m = mesh.shape["row"], mesh.shape["col"]
    placed = (
        P("row", "col", None, None),
        P("row", None, "col", None),
        P("col", None, "row", None),
        P(None, "col", "row", None),
        P(None, "row", "col", None),
        P("row"),
        P("col"),
        P(),
    )
    exchanged = m == 2 and n == 16
    return jax.shard_map(
        exchange_body if exchanged else gather_body,
        mesh=mesh,
        in_specs=placed,
        out_specs=P("row", "col", None, None),
        check_vma=False,
    )
```

```python
import functools

import jax
import jax.numpy as jnp
from jax import lax
from jax.experimental import pallas as pl
from jax.experimental.pallas import tpu as pltpu
from jax.sharding import PartitionSpec as P


F32 = jnp.float32
BF16 = jnp.bfloat16
TILE = 256
WIDE = 60


def tile_of(rows):
    return TILE if rows % TILE == 0 else TILE // 2


def any_specs(count):
    return [pl.BlockSpec(memory_space=pl.ANY)] * count


def vmem():
    return pl.BlockSpec(memory_space=pltpu.VMEM)


def cost(flops, moved):
    return pl.CostEstimate(flops=int(flops), bytes_accessed=int(moved), transcendentals=0)


def limit(mib):
    return pltpu.CompilerParams(vmem_limit_bytes=mib << 20)


def flipped(block):
    return jnp.transpose(block)


def turn_kernel(wl_ref, *out_refs):
    depth = wl_ref.shape[1]
    first = 0
    for out_ref in out_refs:
        rows = out_ref.shape[0]
        tile = tile_of(rows)
        for k in range(wl_ref.shape[0]):
            @pl.loop(0, rows // tile)
            def _(s):
                at = pl.multiple_of(s * tile, tile)
                block = wl_ref[k, :, pl.ds(first + at, tile)]
                out_ref[pl.ds(at, tile), pl.ds(k * depth, depth)] = flipped(block)
        first += rows


def turn(wl, heights):
    panels, depth, _ = wl.shape
    return pl.pallas_call(
        turn_kernel,
        out_shape=[jax.ShapeDtypeStruct((rows, panels * depth), BF16) for rows in heights],
        in_specs=[vmem()],
        out_specs=[vmem()] * len(heights),
        compiler_params=limit(8),
        cost_estimate=cost(0, 4 * wl.size),
        name="turn",
    )(wl)


def gather_copies(pieces, dst, sem):
    me = lax.axis_index("row")
    out = []
    for n, piece in enumerate(pieces):
        rows = piece.shape[1]
        at = pl.multiple_of((me ^ n) * rows, rows)
        out.append(pltpu.make_async_copy(piece, dst.at[:, pl.ds(at, rows), :], sem.at[n]))
    return out


def hbm():
    return pl.BlockSpec(memory_space=pltpu.HBM)


def mirror_mix_kernel(*refs):
    *pieces, mine_ref, theirs_ref, right, mixed, sem, side = refs
    panels, virt, _ = right.shape
    half = virt // 2
    y = lax.axis_index("col")
    mine = pl.multiple_of(y * half, half)
    theirs = pl.multiple_of((1 - y) * half, half)
    copies = gather_copies(pieces, right, sem)
    for copy in copies:
        copy.start()
    for copy in copies:
        copy.wait()
    blocks = virt // TILE
    out = []
    for k in range(panels):
        @pl.loop(0, blocks * blocks)
        def _(s):
            up = pl.multiple_of((s // blocks) * TILE, TILE)
            along = pl.multiple_of((s % blocks) * TILE, TILE)
            across = flipped(right[k, pl.ds(along, TILE), pl.ds(up, TILE)]).astype(F32)
            here = right[k, pl.ds(up, TILE), pl.ds(along, TILE)].astype(F32)
            mixed[k, pl.ds(up, TILE), pl.ds(along, TILE)] = (2.0 * across - here).astype(BF16)

        for n, (at, dst) in enumerate(((mine, mine_ref), (theirs, theirs_ref))):
            out.append(
                pltpu.make_async_copy(mixed.at[k, pl.ds(at, half), :], dst.at[k], side.at[2 * k + n])
            )
            out[-1].start()
    for copy in out:
        copy.wait()


def mirror_mix(pieces, panels, virt):
    return pl.pallas_call(
        mirror_mix_kernel,
        out_shape=[jax.ShapeDtypeStruct((panels, virt // 2, virt), BF16)] * 2,
        in_specs=any_specs(len(pieces)),
        out_specs=[hbm(), hbm()],
        scratch_shapes=[
            pltpu.VMEM((panels, virt, virt), BF16),
            pltpu.VMEM((panels, virt, virt), BF16),
            pltpu.SemaphoreType.DMA((len(pieces),)),
            pltpu.SemaphoreType.DMA((2 * panels,)),
        ],
        compiler_params=limit(WIDE),
        cost_estimate=cost(0, 8 * virt * virt),
        name="mirror_mix",
    )(*pieces)


def direct_kernel(heights, *refs):
    *refs, own_ref, other_ref, mine_ref, out_ref, weight, own, other, mixed, turned, sem, came, side = refs
    pieces, blocks = refs[: -len(heights)], refs[-len(heights):]
    panels, virt, _ = weight.shape
    half = virt // 2
    first = [pltpu.make_async_copy(mine_ref, mixed, side.at[0])]
    at = 0
    for n, (rows, block) in enumerate(zip(heights, blocks)):
        first.append(pltpu.make_async_copy(block, turned.at[pl.ds(at, rows)], came.at[n]))
        at += rows
    then = gather_copies(pieces, weight, sem)
    then.append(pltpu.make_async_copy(own_ref, own, side.at[1]))
    then.append(pltpu.make_async_copy(other_ref, other, side.at[2]))
    for copy in first + then:
        copy.start()
    for copy in first:
        copy.wait()

    @pl.loop(0, virt // TILE)
    def _(s):
        span = pl.ds(pl.multiple_of(s * TILE, TILE), TILE)
        part = jnp.zeros((TILE, virt), F32)
        for k in range(panels):
            part += jnp.dot(turned[span, pl.ds(k * half, half)], mixed[k], preferred_element_type=F32)
        out_ref[span, :] = part

    for copy in then:
        copy.wait()
    y = lax.axis_index("col")
    mine = pl.multiple_of(y * half, half)
    theirs = pl.multiple_of((1 - y) * half, half)
    for rows_ref, start in ((own, mine), (other, theirs)):
        @pl.loop(0, half // TILE)
        def _(s):
            at = pl.multiple_of(s * TILE, TILE)
            span = pl.ds(pl.multiple_of(start + at, TILE), TILE)
            part = out_ref[span, :]
            for k in range(panels):
                for columns_ref, inner in ((own, mine), (other, theirs)):
                    here = rows_ref[k, pl.ds(at, TILE), pl.ds(inner, half)].astype(F32)
                    across = flipped(columns_ref[k, :, span]).astype(F32)
                    left = (2.0 * here - across).astype(BF16)
                    part += jnp.dot(left, weight[k, pl.ds(inner, half), :], preferred_element_type=F32)
            out_ref[span, :] = part


def direct_part(pieces, heights, turned, own, other, mine):
    panels, half, virt = own.shape
    side = pltpu.VMEM((panels, half, virt), BF16)
    return pl.pallas_call(
        functools.partial(direct_kernel, heights),
        out_shape=jax.ShapeDtypeStruct((virt, virt), F32),
        in_specs=any_specs(len(pieces) + len(heights) + 3),
        out_specs=vmem(),
        scratch_shapes=[
            pltpu.VMEM((panels, virt, virt), BF16),
            side,
            side,
            side,
            pltpu.VMEM((virt, panels * half), BF16),
            pltpu.SemaphoreType.DMA((len(pieces),)),
            pltpu.SemaphoreType.DMA((len(heights),)),
            pltpu.SemaphoreType.DMA((3,)),
        ],
        compiler_params=limit(24),
        cost_estimate=cost(3 * panels * virt**3, 14 * virt * virt),
        name="direct_part",
    )(*pieces, *turned, own, other, mine)


def strip_of(rows, virt):
    return virt if rows > TILE else virt // 2


def finish_kernel(first, el_ref, er_ref, evr_ref, evc_ref, base_ref, amp_ref, came_ref, mixed_ref, *rest):
    out_ref, done, sem = rest[-3:]
    panels, half, virt = mixed_ref.shape
    rows = came_ref.shape[0]
    level = el_ref[0] + er_ref[0]
    tile = tile_of(rows)
    width = strip_of(rows, virt)
    copies = []
    for at in range(0, rows, tile):
        copies += [
            pltpu.make_async_copy(
                done.at[pl.ds(at, tile), pl.ds(along, width)],
                out_ref.at[pl.ds(first + at, tile), pl.ds(along, width)],
                sem.at[at // tile, along // width],
            )
            for along in range(0, virt, width)
        ]
        down = evc_ref[pl.ds(first + at, tile), :]
        for along in range(0, virt, width):
            strip = pl.ds(along, width)
            total = base_ref[pl.ds(first + at, tile), strip]
            for k in range(panels):
                total += jnp.dot(
                    came_ref[pl.ds(at, tile), pl.ds(k * half, half)],
                    mixed_ref[k, :, strip],
                    preferred_element_type=F32,
                )
            pair = down + evr_ref[:, strip]
            before = amp_ref[pl.ds(first + at, tile), strip]
            done[pl.ds(at, tile), strip] = before + total / (level - pair)
            copies[at // tile * (virt // width) + along // width].start()
    for copy in copies:
        copy.wait()


def finish(first, el, er, evr, evc, base, amp, came, mixed, held):
    virt = base.shape[0]
    panels = mixed.shape[0]
    rows = came.shape[0]
    width = strip_of(rows, virt)
    smem = pl.BlockSpec(memory_space=pltpu.SMEM)
    in_specs = [smem] * 2 + [vmem()] * 6
    args = [el, er, evr, evc, base, amp, came, mixed]
    aliases = {}
    if held is not None:
        in_specs.append(pl.BlockSpec(memory_space=pl.ANY))
        args.append(held)
        aliases = {len(args) - 1: 0}
    return pl.pallas_call(
        functools.partial(finish_kernel, first),
        out_shape=jax.ShapeDtypeStruct((virt, virt), F32),
        in_specs=in_specs,
        out_specs=pl.BlockSpec(memory_space=pl.ANY),
        input_output_aliases=aliases,
        scratch_shapes=[pltpu.VMEM((rows, virt), F32), pltpu.SemaphoreType.DMA((rows // tile_of(rows), virt // width))],
        compiler_params=limit(8),
        cost_estimate=cost(panels * rows * virt * virt, 12 * rows * virt + 4 * virt * virt),
        name="finish",
    )(*args)


def exchange_body(
    amplitudes,
    panels_left,
    panels_right,
    weights_right,
    weights_left,
    energy_left,
    energy_right,
    energy_virtual,
):
    n = lax.axis_size("row")
    own = panels_left[0]
    panels, _, virt = own.shape
    heights = (7 * virt // 8, virt // 8)

    def over_col(block):
        return lax.ppermute(block, "col", [(0, 1), (1, 0)])

    def over_row(block, across, steps=range(4)):
        return lax.ppermute(block, "row", [(r, r ^ across) for r in range(n) if r // 4 in steps])

    other = over_col(own)
    turned = turn(weights_left[:, 0], heights)
    came = [over_col(block) for block in turned]
    inner = (lax.axis_index("row") // 4) % 3 > 0
    gathered = []
    for shard in (panels_right[0], weights_right[:, 0]):
        by_step = [shard, over_row(shard, 4), over_row(shard, 8)]
        middle = over_row(shard, 12, (1, 2))
        ends = over_row(by_step[2], 4, (1, 2))
        by_step.append(jnp.where(inner, middle, ends))
        pieces = []
        for piece in by_step:
            across = over_row(piece, 2)
            for block in (piece, across):
                pieces += [block, over_row(block, 1)]
        gathered.append(pieces)
    mine, mixed = mirror_mix(gathered[0], panels, virt)
    base = direct_part(gathered[1], heights, turned, own, other, mine)
    out = None
    first = 0
    for rows, block in zip(heights, came):
        out = finish(
            first,
            energy_left,
            energy_right,
            energy_virtual[None, :],
            energy_virtual[:, None],
            base,
            amplitudes[0, 0],
            block,
            mixed,
            out,
        )
        first += rows
    return out[None, None]


def combine_blocks(blocks):
    as_float = blocks.astype(F32)
    return (2.0 * as_float - jnp.swapaxes(as_float, -1, -2)).astype(BF16)


def gather_body(
    amplitudes,
    panels_left,
    panels_right,
    weights_right,
    weights_left,
    energy_left,
    energy_right,
    energy_virtual,
):
    left_mixed = combine_blocks(lax.all_gather(panels_left[0], "col", axis=1, tiled=True))
    right_mixed = combine_blocks(lax.all_gather(panels_right[0], "row", axis=1, tiled=True))
    weight_right = lax.all_gather(weights_right[:, 0], "row", axis=1, tiled=True)
    weight_left = lax.all_gather(weights_left[:, 0], "col", axis=1, tiled=True)
    direct = jnp.einsum("kac,kcb->ab", left_mixed, weight_right, preferred_element_type=F32)
    mirror = jnp.einsum("kac,kcb->ab", right_mixed, weight_left, preferred_element_type=F32)
    residual = direct + jnp.transpose(mirror)
    virt_pair = energy_virtual[:, None] + energy_virtual[None, :]
    denominator = energy_left[0] + energy_right[0] - virt_pair
    return (amplitudes[0, 0] + residual / denominator)[None, None]


def solution(mesh):
    n, m = mesh.shape["row"], mesh.shape["col"]
    placed = (
        P("row", "col", None, None),
        P("row", None, "col", None),
        P("col", None, "row", None),
        P(None, "col", "row", None),
        P(None, "row", "col", None),
        P("row"),
        P("col"),
        P(),
    )
    exchanged = m == 2 and n == 16
    return jax.shard_map(
        exchange_body if exchanged else gather_body,
        mesh=mesh,
        in_specs=placed,
        out_specs=P("row", "col", None, None),
        check_vma=False,
    )
```

```python
import functools

import jax
import jax.numpy as jnp
from jax import lax
from jax.experimental import pallas as pl
from jax.experimental.pallas import tpu as pltpu
from jax.sharding import PartitionSpec as P


F32 = jnp.float32
BF16 = jnp.bfloat16
TILE = 256
WIDE = 60
STRIP = 1024


def tile_of(rows):
    return TILE if rows % TILE == 0 else TILE // 2


def any_specs(count):
    return [pl.BlockSpec(memory_space=pl.ANY)] * count


def vmem():
    return pl.BlockSpec(memory_space=pltpu.VMEM)


def cost(flops, moved):
    return pl.CostEstimate(flops=int(flops), bytes_accessed=int(moved), transcendentals=0)


def limit(mib):
    return pltpu.CompilerParams(vmem_limit_bytes=mib << 20)


def flipped(block):
    return jnp.transpose(block)


def turn_kernel(wl_ref, *out_refs):
    depth = wl_ref.shape[1]
    first = 0
    for out_ref in out_refs:
        rows = out_ref.shape[0]
        tile = tile_of(rows)
        for k in range(wl_ref.shape[0]):
            @pl.loop(0, rows // tile)
            def _(s):
                at = pl.multiple_of(s * tile, tile)
                block = wl_ref[k, :, pl.ds(first + at, tile)]
                out_ref[pl.ds(at, tile), pl.ds(k * depth, depth)] = flipped(block)
        first += rows


def turn(wl, heights):
    panels, depth, _ = wl.shape
    return pl.pallas_call(
        turn_kernel,
        out_shape=[jax.ShapeDtypeStruct((rows, panels * depth), BF16) for rows in heights],
        in_specs=[vmem()],
        out_specs=[vmem()] * len(heights),
        compiler_params=limit(8),
        cost_estimate=cost(0, 4 * wl.size),
        name="turn",
    )(wl)


def gather_copies(pieces, dst, sem):
    me = lax.axis_index("row")
    out = []
    for n, piece in enumerate(pieces):
        rows = piece.shape[1]
        at = pl.multiple_of((me ^ n) * rows, rows)
        out.append(pltpu.make_async_copy(piece, dst.at[:, pl.ds(at, rows), :], sem.at[n]))
    return out


def hbm():
    return pl.BlockSpec(memory_space=pltpu.HBM)


def mirror_mix_kernel(*refs):
    *pieces, mine_ref, theirs_ref, right, mixed, sem, side = refs
    panels, virt, _ = right.shape
    half = virt // 2
    y = lax.axis_index("col")
    mine = pl.multiple_of(y * half, half)
    theirs = pl.multiple_of((1 - y) * half, half)
    copies = gather_copies(pieces, right, sem)
    for copy in copies:
        copy.start()
    for copy in copies:
        copy.wait()
    blocks = virt // TILE
    out = []
    for k in range(panels):
        @pl.loop(0, blocks * blocks)
        def _(s):
            up = pl.multiple_of((s // blocks) * TILE, TILE)
            along = pl.multiple_of((s % blocks) * TILE, TILE)
            across = flipped(right[k, pl.ds(along, TILE), pl.ds(up, TILE)]).astype(F32)
            here = right[k, pl.ds(up, TILE), pl.ds(along, TILE)].astype(F32)
            mixed[k, pl.ds(up, TILE), pl.ds(along, TILE)] = (2.0 * across - here).astype(BF16)

        for n, (at, dst) in enumerate(((mine, mine_ref), (theirs, theirs_ref))):
            out.append(
                pltpu.make_async_copy(mixed.at[k, pl.ds(at, half), :], dst.at[k], side.at[2 * k + n])
            )
            out[-1].start()
    for copy in out:
        copy.wait()


def mirror_mix(pieces, panels, virt):
    return pl.pallas_call(
        mirror_mix_kernel,
        out_shape=[jax.ShapeDtypeStruct((panels, virt // 2, virt), BF16)] * 2,
        in_specs=any_specs(len(pieces)),
        out_specs=[hbm(), hbm()],
        scratch_shapes=[
            pltpu.VMEM((panels, virt, virt), BF16),
            pltpu.VMEM((panels, virt, virt), BF16),
            pltpu.SemaphoreType.DMA((len(pieces),)),
            pltpu.SemaphoreType.DMA((2 * panels,)),
        ],
        compiler_params=limit(WIDE),
        cost_estimate=cost(0, 8 * virt * virt),
        name="mirror_mix",
    )(*pieces)


def direct_kernel(heights, *refs):
    *refs, own_ref, other_ref, mine_ref, out_ref, weight, own, other, mixed, turned, sem, came, side = refs
    pieces, blocks = refs[: -len(heights)], refs[-len(heights):]
    panels, virt, _ = weight.shape
    half = virt // 2
    first = [pltpu.make_async_copy(mine_ref, mixed, side.at[0])]
    at = 0
    for n, (rows, block) in enumerate(zip(heights, blocks)):
        first.append(pltpu.make_async_copy(block, turned.at[pl.ds(at, rows)], came.at[n]))
        at += rows
    then = gather_copies(pieces, weight, sem)
    then.append(pltpu.make_async_copy(own_ref, own, side.at[1]))
    then.append(pltpu.make_async_copy(other_ref, other, side.at[2]))
    for copy in first + then:
        copy.start()
    for copy in first:
        copy.wait()

    @pl.loop(0, virt // TILE)
    def _(s):
        span = pl.ds(pl.multiple_of(s * TILE, TILE), TILE)
        part = jnp.zeros((TILE, virt), F32)
        for k in range(panels):
            part += jnp.dot(turned[span, pl.ds(k * half, half)], mixed[k], preferred_element_type=F32)
        out_ref[span, :] = part

    for copy in then:
        copy.wait()
    y = lax.axis_index("col")
    mine = pl.multiple_of(y * half, half)
    theirs = pl.multiple_of((1 - y) * half, half)
    for rows_ref, start in ((own, mine), (other, theirs)):
        @pl.loop(0, half // TILE)
        def _(s):
            at = pl.multiple_of(s * TILE, TILE)
            span = pl.ds(pl.multiple_of(start + at, TILE), TILE)
            part = out_ref[span, :]
            for k in range(panels):
                for columns_ref, inner in ((own, mine), (other, theirs)):
                    here = rows_ref[k, pl.ds(at, TILE), pl.ds(inner, half)].astype(F32)
                    across = flipped(columns_ref[k, :, span]).astype(F32)
                    left = (2.0 * here - across).astype(BF16)
                    part += jnp.dot(left, weight[k, pl.ds(inner, half), :], preferred_element_type=F32)
            out_ref[span, :] = part


def direct_part(pieces, heights, turned, own, other, mine):
    panels, half, virt = own.shape
    side = pltpu.VMEM((panels, half, virt), BF16)
    return pl.pallas_call(
        functools.partial(direct_kernel, heights),
        out_shape=jax.ShapeDtypeStruct((virt, virt), F32),
        in_specs=any_specs(len(pieces) + len(heights) + 3),
        out_specs=vmem(),
        scratch_shapes=[
            pltpu.VMEM((panels, virt, virt), BF16),
            side,
            side,
            side,
            pltpu.VMEM((virt, panels * half), BF16),
            pltpu.SemaphoreType.DMA((len(pieces),)),
            pltpu.SemaphoreType.DMA((len(heights),)),
            pltpu.SemaphoreType.DMA((3,)),
        ],
        compiler_params=limit(24),
        cost_estimate=cost(3 * panels * virt**3, 14 * virt * virt),
        name="direct_part",
    )(*pieces, *turned, own, other, mine)


def finish_kernel(first, el_ref, er_ref, evr_ref, evc_ref, base_ref, amp_ref, came_ref, mixed_ref, *rest):
    out_ref, done, sem = rest[-3:]
    panels, half, virt = mixed_ref.shape
    rows = came_ref.shape[0]
    level = el_ref[0] + er_ref[0]
    tile = tile_of(rows)
    copies = []
    for at in range(0, rows, tile):
        copies += [
            pltpu.make_async_copy(
                done.at[pl.ds(at, tile), pl.ds(along, STRIP)],
                out_ref.at[pl.ds(first + at, tile), pl.ds(along, STRIP)],
                sem.at[at // tile, along // STRIP],
            )
            for along in range(0, virt, STRIP)
        ]
        down = evc_ref[pl.ds(first + at, tile), :]
        for along in range(0, virt, STRIP):
            strip = pl.ds(along, STRIP)
            total = base_ref[pl.ds(first + at, tile), strip]
            for k in range(panels):
                total += jnp.dot(
                    came_ref[pl.ds(at, tile), pl.ds(k * half, half)],
                    mixed_ref[k, :, strip],
                    preferred_element_type=F32,
                )
            pair = down + evr_ref[:, strip]
            before = amp_ref[pl.ds(first + at, tile), strip]
            done[pl.ds(at, tile), strip] = before + total / (level - pair)
            copies[at // tile * (virt // STRIP) + along // STRIP].start()
    for copy in copies:
        copy.wait()


def finish(first, el, er, evr, evc, base, amp, came, mixed, held):
    virt = base.shape[0]
    panels = mixed.shape[0]
    rows = came.shape[0]
    smem = pl.BlockSpec(memory_space=pltpu.SMEM)
    in_specs = [smem] * 2 + [vmem()] * 6
    args = [el, er, evr, evc, base, amp, came, mixed]
    aliases = {}
    if held is not None:
        in_specs.append(pl.BlockSpec(memory_space=pl.ANY))
        args.append(held)
        aliases = {len(args) - 1: 0}
    return pl.pallas_call(
        functools.partial(finish_kernel, first),
        out_shape=jax.ShapeDtypeStruct((virt, virt), F32),
        in_specs=in_specs,
        out_specs=pl.BlockSpec(memory_space=pl.ANY),
        input_output_aliases=aliases,
        scratch_shapes=[pltpu.VMEM((rows, virt), F32), pltpu.SemaphoreType.DMA((rows // tile_of(rows), virt // STRIP))],
        compiler_params=limit(8),
        cost_estimate=cost(panels * rows * virt * virt, 12 * rows * virt + 4 * virt * virt),
        name="finish",
    )(*args)


def exchange_body(
    amplitudes,
    panels_left,
    panels_right,
    weights_right,
    weights_left,
    energy_left,
    energy_right,
    energy_virtual,
):
    n = lax.axis_size("row")
    own = panels_left[0]
    panels, _, virt = own.shape
    heights = (7 * virt // 8, virt // 8)

    def over_col(block):
        return lax.ppermute(block, "col", [(0, 1), (1, 0)])

    def over_row(block, across, steps=range(4)):
        return lax.ppermute(block, "row", [(r, r ^ across) for r in range(n) if r // 4 in steps])

    other = over_col(own)
    turned = turn(weights_left[:, 0], heights)
    came = [over_col(block) for block in turned]
    inner = (lax.axis_index("row") // 4) % 3 > 0
    gathered = []
    for shard in (panels_right[0], weights_right[:, 0]):
        by_step = [shard, over_row(shard, 4), over_row(shard, 8)]
        middle = over_row(shard, 12, (1, 2))
        ends = over_row(by_step[2], 4, (1, 2))
        by_step.append(jnp.where(inner, middle, ends))
        pieces = []
        for piece in by_step:
            across = over_row(piece, 2)
            for block in (piece, across):
                pieces += [block, over_row(block, 1)]
        gathered.append(pieces)
    mine, mixed = mirror_mix(gathered[0], panels, virt)
    base = direct_part(gathered[1], heights, turned, own, other, mine)
    out = None
    first = 0
    for rows, block in zip(heights, came):
        out = finish(
            first,
            energy_left,
            energy_right,
            energy_virtual[None, :],
            energy_virtual[:, None],
            base,
            amplitudes[0, 0],
            block,
            mixed,
            out,
        )
        first += rows
    return out[None, None]


def combine_blocks(blocks):
    as_float = blocks.astype(F32)
    return (2.0 * as_float - jnp.swapaxes(as_float, -1, -2)).astype(BF16)


def gather_body(
    amplitudes,
    panels_left,
    panels_right,
    weights_right,
    weights_left,
    energy_left,
    energy_right,
    energy_virtual,
):
    left_mixed = combine_blocks(lax.all_gather(panels_left[0], "col", axis=1, tiled=True))
    right_mixed = combine_blocks(lax.all_gather(panels_right[0], "row", axis=1, tiled=True))
    weight_right = lax.all_gather(weights_right[:, 0], "row", axis=1, tiled=True)
    weight_left = lax.all_gather(weights_left[:, 0], "col", axis=1, tiled=True)
    direct = jnp.einsum("kac,kcb->ab", left_mixed, weight_right, preferred_element_type=F32)
    mirror = jnp.einsum("kac,kcb->ab", right_mixed, weight_left, preferred_element_type=F32)
    residual = direct + jnp.transpose(mirror)
    virt_pair = energy_virtual[:, None] + energy_virtual[None, :]
    denominator = energy_left[0] + energy_right[0] - virt_pair
    return (amplitudes[0, 0] + residual / denominator)[None, None]


def solution(mesh):
    n, m = mesh.shape["row"], mesh.shape["col"]
    placed = (
        P("row", "col", None, None),
        P("row", None, "col", None),
        P("col", None, "row", None),
        P(None, "col", "row", None),
        P(None, "row", "col", None),
        P("row"),
        P("col"),
        P(),
    )
    exchanged = m == 2 and n == 16
    return jax.shard_map(
        exchange_body if exchanged else gather_body,
        mesh=mesh,
        in_specs=placed,
        out_specs=P("row", "col", None, None),
        check_vma=False,
    )
```
